256 devices in a mesh: row: 16 (over x, z_lo, core), col: 16 (over z_hi, y).
Axes of the slice: x: 4, y: 4, z: 8 (z_hi: 4, z_lo: 2; z = z_hi * 2 + z_lo), core: 2. Of those that a mesh axis runs over, the one named last changes fastest.
Arguments:
- tokens: bfloat16 [2048, 2048], P('col'), may hold values from -6 to 6
- left_proj: bfloat16 [2048, 4096], P(None, 'row'), may hold values from -0.09375 to 0.09375
- teacher_up: bfloat16 [4096, 14848], P('row', 'col'), may hold values from -0.09375 to 0.09375
- right_proj: bfloat16 [14848, 7424], P('col', 'row'), may hold values from -0.046875 to 0.046875
- student_gate: bfloat16 [2048, 7424], P(None, 'row'), may hold values from -0.125 to 0.125
- target: bfloat16 [2048, 7424], P('col', 'row'), may hold values from -5 to 5
Outputs:
- grad_left: float32 [2048, 4096], P('col', 'row')
- grad_right: float32 [14848, 7424], P('col', 'row')
The draws below stay inside these ranges and needn't reach their ends.
All inputs are finite; a program needn't handle non-finite values.
Results may differ from the reference program's by a relative error of at most 0.017.
Values may be sent and summed in bfloat16 or wider, within the bound.
No kernel may reach another device: no remote copies, remote signals or barrier semaphores. Data moves between devices by JAX's collectives and lax.ppermute only.
A program may use at most 64 MiB of HBM per device.

```python
import math
import jax
import jax.numpy as jnp
from jax import lax

D_TEACH = 4096
F_TEACH = 14848
D_STU = 2048
F_STU = 7424
TOKENS = 2048
N_ROW = 16


def level_of(stream_key, extent, pieces, least, top_value):
    loudness = 1.0
    for dim, blocks in pieces:
        heights = jax.random.uniform(jax.random.fold_in(jax.random.fold_in(stream_key, 6), dim), (blocks,), jnp.float32, least / len(pieces), top_value / len(pieces))
        loudness = loudness * jnp.repeat(jnp.exp(heights), extent[dim] // blocks).reshape((-1,) + (1,) * (len(extent) - 1 - dim))
    return loudness


def noise(own_key, shape, deviation, reach, shards=(), kind=jnp.bfloat16):
    factor_of = level_of(own_key, shape, shards, -0.22, 0.18) if shards else 1.0
    drawn = jax.random.normal(own_key, shape, jnp.float32) * deviation * factor_of
    return jnp.minimum(jnp.maximum(drawn, -reach), reach).astype(kind)


def setup_inputs(seed: int = 0) -> dict:
    key_list = jax.random.split(jax.random.key(seed), 7)
    return {
        "tokens": noise(key_list[0], (TOKENS, D_STU), 1.0, 6.0, ((0, 16),)),
        "left_proj": noise(key_list[1], (D_STU, D_TEACH), D_TEACH ** -0.5, 0.09375, ((1, 16),)),
        "teacher_up": noise(key_list[2], (D_TEACH, F_TEACH), D_TEACH ** -0.5, 0.09375, ((0, 16), (1, 16))),
        "right_proj": noise(key_list[3], (F_TEACH, F_STU), F_TEACH ** -0.5, 0.046875, ((0, 16), (1, 16))),
        "student_gate": noise(key_list[4], (D_STU, F_STU), D_STU ** -0.5, 0.125, ((1, 16),)),
        "target": noise(key_list[5], (TOKENS, F_STU), 1.0, 5.0, ((0, 16), (1, 16))),
    }


def block_sum(first_factor, second_factor, blocks):
    block_width = first_factor.shape[1] // blocks
    first_blocks = first_factor.reshape(first_factor.shape[0], blocks, block_width).transpose(1, 0, 2)
    second_blocks = second_factor.reshape(blocks, block_width, second_factor.shape[1])

    def advance(running, operands):
        partial_value = jnp.dot(operands[0], operands[1], preferred_element_type=jnp.float32)
        partial_value = lax.optimization_barrier(partial_value.astype(jnp.bfloat16)).astype(jnp.float32)
        return (running + partial_value, None)
    start_value = jnp.zeros((first_factor.shape[0], second_factor.shape[1]), jnp.float32)
    summed, _ = lax.scan(advance, start_value, (first_blocks, second_blocks))
    return summed

def reference(tokens, left_proj, teacher_up, right_proj, student_gate, target):
    hidden_proj = jnp.dot(left_proj, teacher_up, preferred_element_type=jnp.float32).astype(jnp.bfloat16)
    student_up = jnp.dot(hidden_proj, right_proj, preferred_element_type=jnp.float32).astype(jnp.bfloat16)
    gate_pre = jnp.dot(tokens, student_gate, preferred_element_type=jnp.float32)
    up_pre = jnp.dot(tokens, student_up, preferred_element_type=jnp.float32)
    gate_act = jax.nn.silu(gate_pre)
    factor = 1.0 / math.sqrt(TOKENS)
    grad_up = ((gate_act * up_pre - target.astype(jnp.float32)) * gate_act * factor).astype(jnp.bfloat16)
    grad_student = jnp.dot(tokens.T, grad_up, preferred_element_type=jnp.float32).astype(jnp.bfloat16)
    grad_right = jnp.dot(hidden_proj.T, grad_student, preferred_element_type=jnp.float32)
    grad_hidden = block_sum(grad_student, right_proj.T, N_ROW).astype(jnp.bfloat16)
    grad_left = jnp.dot(grad_hidden, teacher_up.T, preferred_element_type=jnp.float32)
    return (grad_left, grad_right)
```

```python
import math

import jax
import jax.numpy as jnp
from jax import lax
from jax.sharding import PartitionSpec as P

F32 = jnp.float32
BF16 = jnp.bfloat16


def up_gradient(gate_pre, up_pre, target, factor):
    gate_act = jax.nn.silu(gate_pre)
    return ((gate_act * up_pre - target.astype(F32)) * gate_act * factor).astype(BF16)


def send_y(v, d):
    return lax.ppermute(v, "col", [(4 * a + b, 4 * a + (b + d) % 4) for a in range(4) for b in range(4)])


def send_z(v, d):
    return lax.ppermute(v, "col", [(4 * a + b, 4 * ((a + d) % 4) + b) for a in range(4) for b in range(4)])


def send_x(v, d):
    return lax.ppermute(v, "row", [(4 * a + b, 4 * ((a + d) % 4) + b) for a in range(4) for b in range(4)])


def swap_core(v):
    return lax.ppermute(v, "row", [(i, i ^ 1) for i in range(16)])


def swap_zlo(v):
    return lax.ppermute(v, "row", [(i, i ^ 2) for i in range(16)])


def transpose_devices(v, flip):
    pairs = [(16 * r + c, 16 * c + (r ^ flip)) for r in range(16) for c in range(16)]
    return lax.ppermute(v, ("row", "col"), pairs)


def pick(v, i, axis):
    return lax.dynamic_index_in_dim(v, i, axis, keepdims=False)


def put(buf, v, *index):
    v = v.reshape((1,) * len(index) + v.shape)
    return lax.dynamic_update_slice(buf, v, tuple(index) + (0,) * (buf.ndim - len(index)))


def dot(a, b, ca, cb):
    return lax.dot_general(a, b, ((ca, cb), ((), ())), preferred_element_type=F32)


def reduce_col(make, y, zh):
    came = [send_y(make((y + d) % 4).astype(BF16), d) for d in (1, 2, 3)]
    total = make(y)
    for v in came:
        total = total + v.astype(F32)
    half = total.astype(BF16)
    came = [send_z(pick(half, (zh + d) % 4, 0), d) for d in (1, 2, 3)]
    out = pick(total, zh, 0)
    for v in came:
        out = out + v.astype(F32)
    return out


def gather_col(v, y, zh):
    came = [send_z(v, d) for d in (1, 2, 3)]
    part = jnp.zeros((4,) + v.shape, v.dtype)
    part = put(part, v, zh)
    for d, w in zip((1, 2, 3), came):
        part = put(part, w, (zh - d) % 4)
    came = [send_y(part, d) for d in (1, 2, 3)]
    out = jnp.zeros((4, 4) + v.shape, v.dtype)
    out = lax.dynamic_update_slice(out, part[:, None], (0, y) + (0,) * v.ndim)
    for d, w in zip((1, 2, 3), came):
        out = lax.dynamic_update_slice(out, w[:, None], (0, (y - d) % 4) + (0,) * v.ndim)
    return out


def gather_row(v, x, zl, k):
    from_x = {d: send_x(v, d) for d in (2, 1, 3)}
    other = swap_zlo(v)
    mine = [(0, 0, v), (0, 1, other)]
    mine += [(d, 0, from_x[d]) for d in (1, 3)]
    mine += [(d, 1, send_x(other, d)) for d in (1, 3)]
    mine += [(2, 0, from_x[2]), (2, 1, swap_zlo(from_x[2]))]
    out = jnp.zeros((4, 2, 2) + v.shape, v.dtype)
    for d, flip, w in mine:
        xs, zs = (x - d) % 4, zl ^ flip
        out = put(out, w, xs, zs, k)
        out = put(out, swap_core(w), xs, zs, 1 - k)
    return out


def shards(tokens, left_proj, teacher_up, right_proj, student_gate, target):
    r, c = lax.axis_index("row"), lax.axis_index("col")
    x, zl, k = r // 4, (r // 2) % 2, r % 2
    zh, y = c // 4, c % 4
    n_tok = tokens.shape[0]
    factor = 1.0 / math.sqrt(n_tok * 16)

    first = dot(tokens, left_proj, (1,), (0,)).astype(BF16)
    first = gather_col(transpose_devices(first, 0), y, zh)
    first = first.reshape((16,) + first.shape[2:])

    feat = lax.dynamic_slice(tokens, (0, r * 128), (n_tok, 128))
    feat = lax.all_gather(feat, "col", axis=0, tiled=True)
    feat = transpose_devices(feat, 0)

    gate_pre = dot(tokens, student_gate, (1,), (0,))

    teach = gather_row(teacher_up, x, zl, k)
    teach = teach.reshape((16,) + teacher_up.shape)
    second = dot(first, teach, (0, 2), (0, 1)).astype(BF16)
    second = gather_row(second, x, zl, k)
    second = second.reshape((4, 4) + second.shape[3:])

    teach4 = teach.reshape((4, 4) + teacher_up.shape)
    merged = reduce_col(lambda q: dot(pick(teach4, q, 1), right_proj, (2,), (0,)), y, zh).astype(BF16)

    up_pre = reduce_col(lambda q: dot(pick(second, q, 1), right_proj, (2,), (0,)), y, zh)
    grad_up = up_gradient(gate_pre, up_pre, target, factor)
    grad_all = gather_col(grad_up, y, zh)
    grad_all = grad_all.reshape((16,) + grad_up.shape)

    back = dot(grad_all, merged, (2,), (1,))
    back = back.reshape((4, 2, 2) + back.shape[1:])
    came = swap_core(pick(back, 1 - k, 2).astype(BF16))
    back = pick(back, k, 2) + came.astype(F32)
    half = back.astype(BF16)
    came = [send_x(pick(half, (x + d) % 4, 0), d) for d in (1, 2, 3)]
    back = pick(back, x, 0)
    for v in came:
        back = back + v.astype(F32)
    half = back.astype(BF16)
    back = transpose_devices(pick(half, zl, 0), 0).astype(F32) + transpose_devices(
        pick(half, 1 - zl, 0), 2
    ).astype(F32)
    back = gather_col(back.astype(BF16), y, zh)
    back = back.reshape((-1,) + back.shape[3:])
    grad_left = dot(feat, back, (0,), (0,))

    grad_right = dot(second.reshape((-1,) + second.shape[3:]), grad_all.reshape((-1,) + grad_up.shape[1:]), (0,), (0,))
    return (grad_left, grad_right)


def solution(mesh):
    return jax.shard_map(
        shards,
        mesh=mesh,
        in_specs=(
            P("col", None),
            P(None, "row"),
            P("row", "col"),
            P("col", "row"),
            P(None, "row"),
            P("col", "row"),
        ),
        out_specs=(P("col", "row"), P("col", "row")),
        check_vma=False,
    )
```

```python
import math

import jax
import jax.numpy as jnp
from jax import lax
from jax.sharding import PartitionSpec as P

F32 = jnp.float32
BF16 = jnp.bfloat16


def up_gradient(gate_pre, up_pre, target, factor):
    gate_act = jax.nn.silu(gate_pre)
    return ((gate_act * up_pre - target.astype(F32)) * gate_act * factor).astype(BF16)


def send_y(v, d):
    return lax.ppermute(v, "col", [(4 * a + b, 4 * a + (b + d) % 4) for a in range(4) for b in range(4)])


def send_z(v, d):
    return lax.ppermute(v, "col", [(4 * a + b, 4 * ((a + d) % 4) + b) for a in range(4) for b in range(4)])


def send_x(v, d):
    return lax.ppermute(v, "row", [(4 * a + b, 4 * ((a + d) % 4) + b) for a in range(4) for b in range(4)])


def swap_core(v):
    return lax.ppermute(v, "row", [(i, i ^ 1) for i in range(16)])


def swap_zlo(v):
    return lax.ppermute(v, "row", [(i, i ^ 2) for i in range(16)])


def transpose_devices(v, flip):
    pairs = [(16 * r + c, 16 * c + (r ^ flip)) for r in range(16) for c in range(16)]
    return lax.ppermute(v, ("row", "col"), pairs)


def pick(v, i, axis):
    return lax.dynamic_index_in_dim(v, i, axis, keepdims=False)


def dot(a, b, ca, cb):
    return lax.dot_general(a, b, ((ca, cb), ((), ())), preferred_element_type=F32)


def add_all(total, came):
    for v in came:
        total = total + v.astype(F32)
    return total


def gather_col(v):
    part = jnp.stack([v] + [send_z(v, 4 - j) for j in (1, 2, 3)])
    return jnp.stack([part] + [send_y(part, 4 - i) for i in (1, 2, 3)])


def gather_row(v):
    from_x = {d: send_x(v, d) for d in (2, 1, 3)}
    other = swap_zlo(v)
    near = {0: v, 1: from_x[1], 2: from_x[2], 3: from_x[3]}
    far = {0: other, 1: send_x(other, 1), 3: send_x(other, 3), 2: swap_zlo(from_x[2])}
    blocks = []
    for side in (near, far):
        blocks += [side[d] for d in range(4)]
        blocks += [swap_core(side[d]) for d in range(4)]
    return blocks


def shards(tokens, left_proj, teacher_up, right_proj, student_gate, target):
    r, c = lax.axis_index("row"), lax.axis_index("col")
    x, zl, k, low = r // 4, (r // 2) % 2, r % 2, r % 4
    zh, y = c // 4, c % 4
    n_tok = tokens.shape[0]
    n_stu = student_gate.shape[1]
    factor = 1.0 / math.sqrt(n_tok * 16)

    teach = lax.all_gather(teacher_up, "row", axis=0, tiled=True)

    first = dot(tokens, left_proj, (1,), (0,)).astype(BF16)
    first = gather_col(transpose_devices(first, 0))
    first = jnp.concatenate(
        [pick(pick(first, (j - y) % 4, 0), (i - zh) % 4, 0) for i in range(4) for j in range(4)], axis=1
    )

    feat = tokens.reshape(n_tok, 4, 4, -1)
    feat = jnp.stack([pick(feat, y, 2)] + [send_y(pick(feat, (y - i) % 4, 2), 4 - i) for i in (1, 2, 3)])
    feat = jnp.stack([pick(feat, zh, 2)] + [send_z(pick(feat, (zh - i) % 4, 2), 4 - i) for i in (1, 2, 3)], axis=1)

    gate_pre = dot(tokens, student_gate, (1,), (0,))

    second = dot(first, teach, (1,), (0,)).astype(BF16)
    second, teach = lax.optimization_barrier((second, teach))
    second = jnp.concatenate(gather_row(second), axis=0)

    merged = dot(teach, right_proj, (1,), (0,))
    merged = merged.reshape(4, 4, -1, n_stu)
    parts = merged.astype(BF16)
    merged_came = [send_y(pick(parts, (y + d) % 4, 1), d) for d in (1, 2, 3)]
    merged = pick(merged, y, 1)

    up_pre = dot(second, right_proj, (1,), (0,))
    up_pre = up_pre.reshape(4, 4, n_tok, n_stu)
    parts = up_pre.astype(BF16)
    parts, merged_came, merged = lax.optimization_barrier((parts, merged_came, merged))
    came = [send_y(pick(parts, ((y + d) % 4) ^ low, 0), d) for d in (1, 2, 3)]
    up_pre = add_all(pick(up_pre, y ^ low, 0), came)
    parts = up_pre.astype(BF16)
    came = [send_z(pick(parts, (x - zh - d) % 4, 0), d) for d in (1, 2, 3)]
    up_pre = add_all(pick(up_pre, (x - zh) % 4, 0), came)

    merged = add_all(merged, merged_came)
    parts = merged.astype(BF16)
    came = [send_z(pick(parts, (zh + d) % 4, 0), d) for d in (1, 2, 3)]
    merged = add_all(pick(merged, zh, 0), came).astype(BF16)

    grad_up = up_gradient(gate_pre, up_pre, target, factor)
    grad_all = gather_col(grad_up)

    back = dot(grad_all.reshape(-1, n_stu), merged, (1,), (1,))
    back = back.reshape(2, 2, 4, n_tok, -1)
    bit = (k ^ y) % 2
    came = swap_core(pick(back, 1 - bit, 1).astype(BF16))
    back = add_all(pick(back, bit, 1), [came])
    parts = back.astype(BF16)
    came = [send_x(pick(parts, (x + d - zh) % 4, 1), d) for d in (1, 2, 3)]
    back = add_all(pick(back, (x - zh) % 4, 1), came)
    parts = back.astype(BF16)
    mine = zl ^ (((y + bit) // 2) % 2)
    back = transpose_devices(pick(parts, mine, 0), 0).astype(F32)
    back = back + transpose_devices(pick(parts, 1 - mine, 0), 2).astype(F32)
    back = gather_col(back.astype(BF16))
    grad_left = dot(feat.reshape(-1, feat.shape[-1]), back.reshape(-1, back.shape[-1]), (0,), (0,))

    order = [pick(pick(grad_all, ((e ^ low) - y) % 4, 0), (x - d - zh) % 4, 0) for e in range(4) for d in range(4)]
    grad_right = dot(second, jnp.concatenate(order, axis=0), (0,), (0,))
    return (grad_left, grad_right)


def solution(mesh):
    return jax.shard_map(
        shards,
        mesh=mesh,
        in_specs=(
            P("col", None),
            P(None, "row"),
            P("row", "col"),
            P("col", "row"),
            P(None, "row"),
            P("col", "row"),
        ),
        out_specs=(P("col", "row"), P("col", "row")),
        check_vma=False,
    )
```

```python
import math

import jax
import jax.numpy as jnp
from jax import lax
from jax.sharding import PartitionSpec as P

F32 = jnp.float32
BF16 = jnp.bfloat16


def up_gradient(gate_pre, up_pre, target, factor):
    gate_act = jax.nn.silu(gate_pre)
    return ((gate_act * up_pre - target.astype(F32)) * gate_act * factor).astype(BF16)


def send_y(v, d):
    return lax.ppermute(v, "col", [(4 * a + b, 4 * a + (b + d) % 4) for a in range(4) for b in range(4)])


def send_z(v, d):
    return lax.ppermute(v, "col", [(4 * a + b, 4 * ((a + d) % 4) + b) for a in range(4) for b in range(4)])


def send_x(v, d):
    return lax.ppermute(v, "row", [(4 * a + b, 4 * ((a + d) % 4) + b) for a in range(4) for b in range(4)])


def swap_core(v):
    return lax.ppermute(v, "row", [(i, i ^ 1) for i in range(16)])


def swap_zlo(v):
    return lax.ppermute(v, "row", [(i, i ^ 2) for i in range(16)])


def transpose_devices(v, flip):
    pairs = [(16 * r + c, 16 * c + (r ^ flip)) for r in range(16) for c in range(16)]
    return lax.ppermute(v, ("row", "col"), pairs)


def pick(v, i, axis):
    return lax.squeeze(lax.dynamic_slice_in_dim(v, i & jnp.uint32(v.shape[axis] - 1), 1, axis), (axis,))


def dot(a, b, ca, cb):
    return lax.dot_general(a, b, ((ca, cb), ((), ())), preferred_element_type=F32)


def total(own, came):
    out = own.astype(F32)
    for v in came:
        out = out + v.astype(F32)
    return out


def gather_col(v):
    part = jnp.stack([v] + [send_z(v, 4 - j) for j in (1, 2, 3)])
    return jnp.stack([part] + [send_y(part, 4 - i) for i in (1, 2, 3)])


def gather_row(v):
    near = [v] + [send_x(v, d) for d in (1, 2, 3)]
    far = swap_zlo(v)
    far = [far, send_x(far, 1), swap_zlo(near[2]), send_x(far, 3)]
    same = jnp.stack(near + far)
    return same, swap_core(same), near[1]


def shards(tokens, left_proj, teacher_up, right_proj, student_gate, target):
    r, c = lax.axis_index("row").astype(jnp.uint32), lax.axis_index("col").astype(jnp.uint32)
    x, zl, k, low = r >> 2, (r >> 1) & 1, r & 1, r & 3
    zh, y = c >> 2, c & 3
    n_tok = tokens.shape[0]
    n_stu = student_gate.shape[1]
    factor = 1.0 / math.sqrt(n_tok * 16)

    teach = lax.all_gather(teacher_up, "row", axis=0, tiled=True)

    first = dot(tokens, left_proj, (1,), (0,)).astype(BF16)
    first = gather_col(transpose_devices(first, 0))
    first = jnp.concatenate(
        [pick(pick(first, j - y, 0), i - zh, 0) for i in range(4) for j in range(4)], axis=1
    )

    gate_pre = dot(tokens, student_gate, (1,), (0,))

    second = dot(first, teach, (1,), (0,)).astype(BF16)
    same, other, sent = gather_row(second)

    teach, _ = lax.optimization_barrier((teach, sent))
    merged = dot(teach, right_proj, (1,), (0,)).astype(BF16)
    merged = lax.psum_scatter(merged, "col", scatter_dimension=0, tiled=True)

    parts = [dot(v, right_proj, (2,), (0,)).astype(BF16) for v in (same, other)]
    parts = jnp.stack(parts).reshape(2, 2, 4, n_tok, n_stu)

    def part_for(q):
        e = q ^ low
        return pick(pick(parts, e & 1, 0), (e >> 1) & 1, 0)

    came = [send_y(part_for(y + d), d) for d in (1, 2, 3)]
    up_pre = total(part_for(y), came).astype(BF16)
    came = [send_z(pick(up_pre, x - zh - d, 0), d) for d in (1, 2, 3)]
    up_pre = total(pick(up_pre, x - zh, 0), came)

    grad_up = up_gradient(gate_pre, up_pre, target, factor)
    grad_all = gather_col(grad_up)

    back = dot(grad_all, merged, (3,), (1,)).astype(BF16)
    back = back.reshape((2, 2) + back.shape[1:])
    bit = (k ^ y) & 1
    came = swap_core(pick(back, 1 - bit, 1))
    back = total(pick(back, bit, 1), [came]).astype(BF16)
    came = [send_x(pick(back, x + d - zh, 1), d) for d in (1, 2, 3)]
    back = total(pick(back, x - zh, 1), came).astype(BF16)
    mine = zl ^ ((y + bit) >> 1)
    back = total(
        transpose_devices(pick(back, mine, 0), 0), [transpose_devices(pick(back, 1 - mine, 0), 2)]
    ).astype(BF16)
    left = dot(tokens, back, (0,), (0,)).astype(BF16)
    left = left.reshape((4, 4, n_tok) + left.shape[1:])
    came = [send_y(pick(left, y + d, 1), d) for d in (1, 2, 3)]
    left = total(pick(left, y, 1), came).astype(BF16)
    came = [send_z(pick(left, zh + d, 0), d) for d in (1, 2, 3)]
    grad_left = total(pick(left, zh, 0), came)

    def grads_of(e, d):
        return pick(pick(grad_all, (low ^ e) - y, 0), x - d - zh, 0)

    grads = [grads_of(2 * f + h, d) for h in range(2) for f in range(2) for d in range(4)]
    second = jnp.concatenate([same, other]).reshape(-1, same.shape[-1])
    grad_right = dot(second, jnp.concatenate(grads, axis=0), (0,), (0,))
    return (grad_left, grad_right)


def solution(mesh):
    return jax.shard_map(
        shards,
        mesh=mesh,
        in_specs=(
            P("col", None),
            P(None, "row"),
            P("row", "col"),
            P("col", "row"),
            P(None, "row"),
            P("col", "row"),
        ),
        out_specs=(P("col", "row"), P("col", "row")),
        check_vma=False,
    )
```

```python
import math

import jax
import jax.numpy as jnp
from jax import lax
from jax.experimental.layout import Layout, with_layout_constraint
from jax.sharding import PartitionSpec as P

F32 = jnp.float32
BF16 = jnp.bfloat16


def up_gradient(gate_pre, up_pre, target, factor):
    gate_act = jax.nn.silu(gate_pre)
    return ((gate_act * up_pre - target.astype(F32)) * gate_act * factor).astype(BF16)


def send_y(v, d):
    return lax.ppermute(v, "col", [(4 * a + b, 4 * a + (b + d) % 4) for a in range(4) for b in range(4)])


def send_z(v, d):
    return lax.ppermute(v, "col", [(4 * a + b, 4 * ((a + d) % 4) + b) for a in range(4) for b in range(4)])


def send_x(v, d):
    return lax.ppermute(v, "row", [(4 * a + b, 4 * ((a + d) % 4) + b) for a in range(4) for b in range(4)])


def swap_core(v):
    return lax.ppermute(v, "row", [(i, i ^ 1) for i in range(16)])


def swap_zlo(v):
    return lax.ppermute(v, "row", [(i, i ^ 2) for i in range(16)])


def transpose_devices(v, flip):
    pairs = [(16 * r + c, 16 * c + (r ^ flip)) for r in range(16) for c in range(16)]
    return lax.ppermute(v, ("row", "col"), pairs)


def pick(v, i, axis):
    return lax.squeeze(lax.dynamic_slice_in_dim(v, i & jnp.uint32(v.shape[axis] - 1), 1, axis), (axis,))


def dot(a, b, ca, cb):
    return lax.dot_general(a, b, ((ca, cb), ((), ())), preferred_element_type=F32)


def total(own, came):
    out = own.astype(F32)
    for v in came:
        out = out + v.astype(F32)
    return out


def gather_z(v):
    return jnp.stack([v] + [send_z(v, 4 - j) for j in (1, 2, 3)])


def gather_y(v):
    return jnp.stack([v] + [send_y(v, 4 - i) for i in (1, 2, 3)])


def gather_col(v):
    return gather_y(gather_z(v))


def gather_row(v, beside=None):
    near = [v] + [send_x(v, d) for d in (1, 2, 3)]
    far = swap_zlo(v)
    if beside is not None:
        far, beside = lax.optimization_barrier((far, beside))
        beside = gather_z(beside)
    far = [far, send_x(far, 1), swap_zlo(near[2]), send_x(far, 3)]
    if beside is not None:
        near, beside = lax.optimization_barrier((near, beside))
        beside = gather_y(beside)
        far, beside = lax.optimization_barrier((far, beside))
    near, far = jnp.stack(near), jnp.stack(far)
    return [near, swap_core(near), far, swap_core(far)], beside


def shards(tokens, left_proj, teacher_up, right_proj, student_gate, target):
    r, c = lax.axis_index("row").astype(jnp.uint32), lax.axis_index("col").astype(jnp.uint32)
    x, zl, k, low = r >> 2, (r >> 1) & 1, r & 1, r & 3
    zh, y = c >> 2, c & 3
    n_tok = tokens.shape[0]
    n_stu = student_gate.shape[1]
    factor = 1.0 / math.sqrt(n_tok * 16)

    def reduce_y(parts):
        parts = jnp.stack(parts)
        came = [send_y(pick(parts, (y + d) ^ low, 0), d) for d in (1, 2, 3)]
        return pick(parts, y ^ low, 0), came

    def reduce_z(own, came):
        own = total(own, came).astype(BF16)
        came = [send_z(pick(own, x - zh - d, 0), d) for d in (1, 2, 3)]
        return total(pick(own, x - zh, 0), came)

    first = dot(tokens, left_proj, (1,), (0,)).astype(BF16)
    first, teach = lax.optimization_barrier((first, teacher_up))
    teach, first = gather_row(teach, transpose_devices(first, 0))

    def product(e):
        blocks = [pick(pick(first, (low ^ e) - y, 0), x - d - zh, 0) for d in range(4)]
        return dot(jnp.stack(blocks), teach[e], (0, 2), (0, 1))

    second = (product(0) + product(1) + product(2) + product(3)).astype(BF16)
    second, teach = lax.optimization_barrier((second, teach))
    gate_pre = dot(tokens, student_gate, (1,), (0,))
    second, _ = gather_row(second)

    merged, merged_came = reduce_y([dot(v, right_proj, (2,), (0,)).astype(BF16) for v in teach])

    up_pre = [dot(v, right_proj, (2,), (0,)).astype(BF16) for v in second]
    up_pre, merged, merged_came = lax.optimization_barrier((up_pre, merged, merged_came))
    up_pre, came = reduce_y(up_pre)

    second = jnp.stack(second)
    second = [pick(pick(second, low ^ (y + i), 0), x - zh - j, 0) for i in range(4) for j in range(4)]
    second = jnp.stack(second)
    second, up_pre, came = lax.optimization_barrier((second, up_pre, came))

    up_pre = reduce_z(up_pre, came)
    merged = reduce_z(merged, merged_came).astype(BF16)

    grad_up = up_gradient(gate_pre, up_pre, target, factor)
    grad_all = gather_col(grad_up)

    back = dot(grad_all, merged, (3,), (1,)).astype(BF16)
    back = back.reshape((2, 2) + back.shape[1:])
    bit = (k ^ y) & 1
    came = swap_core(pick(back, 1 - bit, 1))
    back = total(pick(back, bit, 1), [came]).astype(BF16)
    came = [send_x(pick(back, x + d - zh, 1), d) for d in (1, 2, 3)]
    back = total(pick(back, x - zh, 1), came).astype(BF16)
    mine = zl ^ ((y + bit) >> 1)
    back = total(
        transpose_devices(pick(back, mine, 0), 0), [transpose_devices(pick(back, 1 - mine, 0), 2)]
    ).astype(BF16)
    left = dot(tokens.reshape(n_tok, 16, -1), back, (0,), (0,)).astype(BF16)
    left = with_layout_constraint(left, Layout(major_to_minor=(0, 1, 2)))
    left = left.reshape((4, 4) + left.shape[1:])
    came = [send_y(pick(left, y + d, 1), d) for d in (1, 2, 3)]
    left = pick(left, y, 1)

    grad_all = grad_all.reshape((16,) + grad_up.shape)
    grad_all, left = lax.optimization_barrier((grad_all, left))
    grad_right = dot(second, grad_all, (0, 1), (0, 1))
    grad_right, left, came = lax.optimization_barrier((grad_right, left, came))

    left = total(left, came).astype(BF16)
    came = [send_z(pick(left, zh + d, 0), d) for d in (1, 2, 3)]
    grad_left = total(pick(left, zh, 0), came)
    return (grad_left, grad_right)


def solution(mesh):
    return jax.shard_map(
        shards,
        mesh=mesh,
        in_specs=(
            P("col", None),
            P(None, "row"),
            P("row", "col"),
            P("col", "row"),
            P(None, "row"),
            P("col", "row"),
        ),
        out_specs=(P("col", "row"), P("col", "row")),
        check_vma=False,
    )
```

```python
import math

import jax
import jax.numpy as jnp
from jax import lax
from jax.experimental.layout import Layout, with_layout_constraint
from jax.sharding import PartitionSpec as P

F32 = jnp.float32
BF16 = jnp.bfloat16


def up_gradient(gate_pre, up_pre, target, factor):
    gate_act = jax.nn.silu(gate_pre)
    return ((gate_act * up_pre - target.astype(F32)) * gate_act * factor).astype(BF16)


def send_y(v, d):
    return lax.ppermute(v, "col", [(4 * a + b, 4 * a + (b + d) % 4) for a in range(4) for b in range(4)])


def send_z(v, d):
    return lax.ppermute(v, "col", [(4 * a + b, 4 * ((a + d) % 4) + b) for a in range(4) for b in range(4)])


def send_x(v, d):
    return lax.ppermute(v, "row", [(4 * a + b, 4 * ((a + d) % 4) + b) for a in range(4) for b in range(4)])


def swap_core(v):
    return lax.ppermute(v, "row", [(i, i ^ 1) for i in range(16)])


def swap_zlo(v):
    return lax.ppermute(v, "row", [(i, i ^ 2) for i in range(16)])


def transpose_devices(v, flip):
    pairs = [(16 * r + c, 16 * c + (r ^ flip)) for r in range(16) for c in range(16)]
    return lax.ppermute(v, ("row", "col"), pairs)


def pick(v, i, axis):
    return lax.squeeze(lax.dynamic_slice_in_dim(v, i & jnp.uint32(v.shape[axis] - 1), 1, axis), (axis,))


def dot(a, b, ca, cb):
    return lax.dot_general(a, b, ((ca, cb), ((), ())), preferred_element_type=F32)


def total(own, came):
    out = own.astype(F32)
    for v in came:
        out = out + v.astype(F32)
    return out


def gather_z(v):
    return jnp.stack([v] + [send_z(v, 4 - j) for j in (1, 2, 3)])


def gather_y(v):
    return jnp.stack([v] + [send_y(v, 4 - i) for i in (1, 2, 3)])


def gather_col(v):
    return gather_y(gather_z(v))


def gather_row(v):
    near = [v] + [send_x(v, d) for d in (1, 2, 3)]
    far = swap_zlo(v)
    far = [far, send_x(far, 1), swap_zlo(near[2]), send_x(far, 3)]
    near, far = jnp.stack(near), jnp.stack(far)
    return [near, swap_core(near), far, swap_core(far)]


def swap_col(v, flip):
    return lax.ppermute(v, "col", [(i, i ^ flip) for i in range(16)])


def pair_up(v, flip):
    return jnp.concatenate([v, swap_col(v, flip)])


def gather_both(v, w):
    near = [v] + [send_x(v, d) for d in (1, 2, 3)]
    far = swap_zlo(v)
    w = transpose_devices(w, 0)[None]
    far, w = lax.optimization_barrier((far, w))
    far = [far, send_x(far, 1), swap_zlo(near[2]), send_x(far, 3)]
    w = pair_up(w, 4)
    near[1], near[3], w = lax.optimization_barrier((near[1], near[3], w))
    w = pair_up(w, 8)
    near, w = lax.optimization_barrier((near, w))
    near = jnp.stack(near)
    near_swapped = swap_core(near)
    w = pair_up(w, 1)
    far, w = lax.optimization_barrier((far, w))
    far = jnp.stack(far)
    w = pair_up(w, 2)
    return [near, near_swapped, far, swap_core(far)], w.reshape((4, 4) + w.shape[1:])


def ring_start(far_block, send):
    h = far_block.shape[0] // 2
    return send(far_block[:h], 1), send(far_block[h:], 3)


def ring_end(after, before, came, send):
    h = after.shape[0] // 2
    after = jnp.concatenate([total(after[:h], [came[0]]).astype(BF16), after[h:]])
    before = jnp.concatenate([before[:h], total(before[h:], [came[1]]).astype(BF16)])
    return send(after, 1), send(before, 3)


def shards(tokens, left_proj, teacher_up, right_proj, student_gate, target):
    r, c = lax.axis_index("row").astype(jnp.uint32), lax.axis_index("col").astype(jnp.uint32)
    x, zl, k, low = r >> 2, (r >> 1) & 1, r & 1, r & 3
    zh, y = c >> 2, c & 3
    n_tok = tokens.shape[0]
    n_stu = student_gate.shape[1]
    factor = 1.0 / math.sqrt(n_tok * 16)

    def reduce_y(parts):
        parts = jnp.stack(parts)
        came = [send_y(pick(parts, (y + d) ^ low, 0), d) for d in (1, 2, 3)]
        return pick(parts, y ^ low, 0), came

    first = dot(tokens, left_proj, (1,), (0,)).astype(BF16)
    first, teach = lax.optimization_barrier((first, teacher_up))
    teach, first = gather_both(teach, first)

    def product(e):
        blocks = [pick(pick(first, low ^ e ^ y, 0), (x - d) ^ zh, 0) for d in range(4)]
        return dot(jnp.stack(blocks), teach[e], (0, 2), (0, 1))

    def block_products(v):
        return dot(v, right_proj, (2,), (0,)).astype(BF16)

    merged = [block_products(v) for v in teach[:2]]
    second = (product(0) + product(1) + product(2) + product(3)).astype(BF16)
    second, teach = lax.optimization_barrier((second, teach))
    gate_pre = dot(tokens, student_gate, (1,), (0,))
    second = gather_row(second)

    merged = jnp.stack(merged + [block_products(v) for v in teach[2:]])
    merged_came = ring_start(pick(merged, (y + 2) ^ low, 0), send_y)

    up_pre, came = reduce_y([block_products(v) for v in second])

    second = jnp.stack(second)
    second = [pick(pick(second, low ^ (y + i), 0), x - zh - j, 0) for i in range(4) for j in range(4)]
    second = jnp.stack(second)
    second, up_pre, came, merged_came = lax.optimization_barrier((second, up_pre, came, merged_came))

    up_pre = total(up_pre, came).astype(BF16)
    came = [send_z(pick(up_pre, x - zh - d, 0), d) for d in (1, 2, 3)]
    merged_came = ring_end(pick(merged, (y + 1) ^ low, 0), pick(merged, (y - 1) ^ low, 0), merged_came, send_y)
    up_pre = total(pick(up_pre, x - zh, 0), came)

    grad_up = up_gradient(gate_pre, up_pre, target, factor)
    grad_all = gather_z(grad_up)
    grad_all, merged_came = lax.optimization_barrier((grad_all, merged_came))
    came = [send_y(grad_all, 4 - i) for i in (1, 2, 3)]
    merged = total(pick(merged, y ^ low, 0), merged_came).astype(BF16)
    merged_came = ring_start(pick(merged, x - zh - 2, 0), send_z)
    came[0], merged_came = lax.optimization_barrier((came[0], merged_came))
    merged_came = ring_end(pick(merged, x - zh - 1, 0), pick(merged, x - zh + 1, 0), merged_came, send_z)
    grad_all = jnp.stack([grad_all] + came)
    merged = total(pick(merged, x - zh, 0), merged_came).astype(BF16)

    back = dot(grad_all, merged, (3,), (1,)).astype(BF16)
    back = back.reshape((2, 2) + back.shape[1:])
    bit = (k ^ y) & 1
    came = swap_core(pick(back, 1 - bit, 1))
    back = total(pick(back, bit, 1), [came]).astype(BF16)
    came = [send_x(pick(back, x + d - zh, 1), d) for d in (1, 2, 3)]
    back = total(pick(back, x - zh, 1), came).astype(BF16)
    mine = zl ^ ((y + bit) >> 1)
    back = total(
        transpose_devices(pick(back, mine, 0), 0), [transpose_devices(pick(back, 1 - mine, 0), 2)]
    ).astype(BF16)
    left = dot(tokens.reshape(n_tok, 16, -1), back, (0,), (0,)).astype(BF16)
    left = with_layout_constraint(left, Layout(major_to_minor=(0, 1, 2)))
    left = left.reshape((4, 4) + left.shape[1:])
    came = [send_y(pick(left, y + d, 1), d) for d in (1, 2, 3)]
    left = pick(left, y, 1)

    grad_all = grad_all.reshape((16,) + grad_up.shape)
    grad_all, left = lax.optimization_barrier((grad_all, left))
    grad_right = dot(second, grad_all, (0, 1), (0, 1))
    grad_right, left, came = lax.optimization_barrier((grad_right, left, came))

    left = total(left, came).astype(BF16)
    came = [send_z(pick(left, zh + d, 0), d) for d in (1, 2, 3)]
    grad_left = total(pick(left, zh, 0), came)
    return (grad_left, grad_right)


def solution(mesh):
    return jax.shard_map(
        shards,
        mesh=mesh,
        in_specs=(
            P("col", None),
            P(None, "row"),
            P("row", "col"),
            P("col", "row"),
            P(None, "row"),
            P("col", "row"),
        ),
        out_specs=(P("col", "row"), P("col", "row")),
        check_vma=False,
    )
```

```python
import math

import jax
import jax.numpy as jnp
from jax import lax
from jax.experimental.layout import Layout, with_layout_constraint
from jax.sharding import PartitionSpec as P

F32 = jnp.float32
BF16 = jnp.bfloat16


def up_gradient(gate_pre, up_pre, target, factor):
    gate_act = jax.nn.silu(gate_pre)
    return ((gate_act * up_pre - target.astype(F32)) * gate_act * factor).astype(BF16)


def send_y(v, d):
    return lax.ppermute(v, "col", [(4 * a + b, 4 * a + (b + d) % 4) for a in range(4) for b in range(4)])


def send_z(v, d):
    return lax.ppermute(v, "col", [(4 * a + b, 4 * ((a + d) % 4) + b) for a in range(4) for b in range(4)])


def send_x(v, d):
    return lax.ppermute(v, "row", [(4 * a + b, 4 * ((a + d) % 4) + b) for a in range(4) for b in range(4)])


def swap_core(v):
    return lax.ppermute(v, "row", [(i, i ^ 1) for i in range(16)])


def swap_zlo(v):
    return lax.ppermute(v, "row", [(i, i ^ 2) for i in range(16)])


def transpose_devices(v, flip):
    pairs = [(16 * r + c, 16 * c + (r ^ flip)) for r in range(16) for c in range(16)]
    return lax.ppermute(v, ("row", "col"), pairs)


def pick(v, i, axis):
    return lax.squeeze(lax.dynamic_slice_in_dim(v, i & jnp.uint32(v.shape[axis] - 1), 1, axis), (axis,))


def dot(a, b, ca, cb):
    return lax.dot_general(a, b, ((ca, cb), ((), ())), preferred_element_type=F32)


def total(own, came):
    out = own.astype(F32)
    for v in came:
        out = out + v.astype(F32)
    return out


def gather_z(v):
    return jnp.stack([v] + [send_z(v, 4 - j) for j in (1, 2, 3)])


def gather_y(v):
    return jnp.stack([v] + [send_y(v, 4 - i) for i in (1, 2, 3)])


def gather_col(v):
    return gather_y(gather_z(v))


def gather_row(v, beside):
    near = [v] + [send_x(v, d) for d in (1, 2, 3)]
    far = swap_zlo(v)
    far = [far, send_x(far, 1), swap_zlo(near[2]), send_x(far, 3)]
    near, beside = lax.optimization_barrier((near, beside))
    near, far = jnp.stack(near), jnp.stack(far)
    return [near, swap_core(near), far, swap_core(far)], beside


def swap_col(v, flip):
    return lax.ppermute(v, "col", [(i, i ^ flip) for i in range(16)])


def pair_up(v, flip):
    return jnp.concatenate([v, swap_col(v, flip)])


def gather_both(v, w):
    near = [v] + [send_x(v, d) for d in (1, 2, 3)]
    far = swap_zlo(v)
    w = transpose_devices(w, 0)[None]
    far, w = lax.optimization_barrier((far, w))
    far = [far, send_x(far, 1), swap_zlo(near[2]), send_x(far, 3)]
    w = pair_up(w, 4)
    near[1], near[3], w = lax.optimization_barrier((near[1], near[3], w))
    w = pair_up(w, 8)
    near, w = lax.optimization_barrier((near, w))
    near = jnp.stack(near)
    near_swapped = swap_core(near)
    w = pair_up(w, 1)
    near_swapped, w = lax.optimization_barrier((near_swapped, w))
    w = pair_up(w, 2)
    far = jnp.stack(far)
    return [near, near_swapped, far, swap_core(far)], w.reshape((4, 4) + w.shape[1:])


def ring_start(far_block, send):
    h = far_block.shape[0] // 2
    return send(far_block[:h], 1), send(far_block[h:], 3)


def ring_end(after, before, came, send):
    h = after.shape[0] // 2
    after = jnp.concatenate([total(after[:h], [came[0]]).astype(BF16), after[h:]])
    before = jnp.concatenate([before[:h], total(before[h:], [came[1]]).astype(BF16)])
    return send(after, 1), send(before, 3)


def shards(tokens, left_proj, teacher_up, right_proj, student_gate, target):
    r, c = lax.axis_index("row").astype(jnp.uint32), lax.axis_index("col").astype(jnp.uint32)
    x, zl, k, low = r >> 2, (r >> 1) & 1, r & 1, r & 3
    zh, y = c >> 2, c & 3
    n_tok = tokens.shape[0]
    n_stu = student_gate.shape[1]
    factor = 1.0 / math.sqrt(n_tok * 16)

    def reduce_y(parts):
        parts = jnp.stack(parts)
        came = [send_y(pick(parts, (y + d) ^ low, 0), d) for d in (1, 2, 3)]
        return pick(parts, y ^ low, 0), came

    feat = lax.dynamic_slice_in_dim(tokens, (2 * x + k) * 256, 256, 1)
    feat = lax.all_gather(feat, "col", axis=0, tiled=True)
    feat = feat.reshape((4, 4) + (n_tok, 256))
    feat = jnp.stack([pick(pick(feat, zh + j, 0), y + i, 0) for i in range(4) for j in range(4)])
    feat = lax.all_gather(feat.reshape(-1, 256), "row", axis_index_groups=[[4 * a + b for a in range(4)] for b in range(4)])

    first = dot(tokens, left_proj, (1,), (0,)).astype(BF16)
    first, teach = lax.optimization_barrier((first, teacher_up))
    teach, first = gather_both(teach, first)

    def product(e):
        blocks = [pick(pick(first, low ^ e ^ y, 0), (x - d) ^ zh, 0) for d in range(4)]
        return dot(jnp.stack(blocks), teach[e], (0, 2), (0, 1))

    def block_products(v):
        return dot(v, right_proj, (2,), (0,)).astype(BF16)

    merged = jnp.stack([block_products(v) for v in teach])
    merged_came = ring_start(pick(merged, (y + 2) ^ low, 0), send_y)
    teach, merged = lax.optimization_barrier((teach, merged))

    second = (product(0) + product(1) + product(2) + product(3)).astype(BF16)
    gate_pre = dot(tokens, student_gate, (1,), (0,))
    second, merged_came = gather_row(second, merged_came)
    merged_came = ring_end(pick(merged, (y + 1) ^ low, 0), pick(merged, (y - 1) ^ low, 0), merged_came, send_y)

    up_pre, came = reduce_y([block_products(v) for v in second])

    second = jnp.stack(second)
    second = [pick(pick(second, low ^ (y + i), 0), x - zh - j, 0) for i in range(4) for j in range(4)]
    second = jnp.stack(second)
    second, up_pre, came, merged_came = lax.optimization_barrier((second, up_pre, came, merged_came))

    up_pre = total(up_pre, came).astype(BF16)
    up_pre, merged_came, feat = lax.optimization_barrier((up_pre, merged_came, feat))
    came = [send_z(pick(up_pre, x - zh - d, 0), d) for d in (1, 2, 3)]
    feat_other = swap_core(feat)
    merged = total(pick(merged, y ^ low, 0), merged_came).astype(BF16)
    came, merged = lax.optimization_barrier((came, merged))
    up_pre = total(pick(up_pre, x - zh, 0), came)

    grad_up = up_gradient(gate_pre, up_pre, target, factor)
    grad_up, merged = lax.optimization_barrier((grad_up, merged))
    grad_all = gather_z(grad_up)
    merged_came = ring_start(pick(merged, x - zh - 2, 0), send_z)
    came = [send_y(grad_all, 4 - i) for i in (1, 2, 3)]
    came[0], merged_came, feat_other = lax.optimization_barrier((came[0], merged_came, feat_other))
    merged_came = ring_end(pick(merged, x - zh - 1, 0), pick(merged, x - zh + 1, 0), merged_came, send_z)
    grad_all = jnp.stack([grad_all] + came)
    grad_all = grad_all.reshape((16,) + grad_up.shape)
    merged = total(pick(merged, x - zh, 0), merged_came).astype(BF16)

    def left_part(v):
        v = v.reshape((4, 16, n_tok, -1))
        v = dot(v, grad_all, (1, 2), (0, 1)).astype(BF16)
        v = dot(v, merged, (2,), (1,)).astype(BF16)
        return v.reshape((4, 2, n_tok, -1))

    left = [left_part(feat), left_part(feat_other)]
    came = swap_core(jnp.stack([pick(left[1], 1 - k, 1), pick(left[0], 1 - k, 1)]))
    left = total(jnp.stack([pick(v, k, 1) for v in left]), [came]).astype(BF16)
    came = [send_x(pick(left, x + d, 1), d) for d in (1, 2, 3)]
    left = total(pick(left, x, 1), came).astype(BF16)

    grad_all, left = lax.optimization_barrier((grad_all, left))
    came = [transpose_devices(pick(left, zl ^ k, 0), 0), transpose_devices(pick(left, 1 - (zl ^ k), 0), 2)]
    grad_right = dot(second, grad_all, (0, 1), (0, 1))
    grad_right, came = lax.optimization_barrier((grad_right, came))
    grad_left = total(came[0], came[1:])
    return (grad_left, grad_right)


def solution(mesh):
    return jax.shard_map(
        shards,
        mesh=mesh,
        in_specs=(
            P("col", None),
            P(None, "row"),
            P("row", "col"),
            P("col", "row"),
            P(None, "row"),
            P("col", "row"),
        ),
        out_specs=(P("col", "row"), P("col", "row")),
        check_vma=False,
    )
```

```python
import math

import jax
import jax.numpy as jnp
from jax import lax
from jax.experimental.layout import Layout, with_layout_constraint
from jax.sharding import PartitionSpec as P

F32 = jnp.float32
BF16 = jnp.bfloat16


def up_gradient(gate_pre, up_pre, target, factor):
    gate_act = jax.nn.silu(gate_pre)
    return ((gate_act * up_pre - target.astype(F32)) * gate_act * factor).astype(BF16)


def send_y(v, d):
    return lax.ppermute(v, "col", [(4 * a + b, 4 * a + (b + d) % 4) for a in range(4) for b in range(4)])


def send_z(v, d):
    return lax.ppermute(v, "col", [(4 * a + b, 4 * ((a + d) % 4) + b) for a in range(4) for b in range(4)])


def send_x(v, d):
    return lax.ppermute(v, "row", [(4 * a + b, 4 * ((a + d) % 4) + b) for a in range(4) for b in range(4)])


def swap_core(v):
    return lax.ppermute(v, "row", [(i, i ^ 1) for i in range(16)])


def swap_zlo(v):
    return lax.ppermute(v, "row", [(i, i ^ 2) for i in range(16)])


def transpose_devices(v, flip):
    pairs = [(16 * r + c, 16 * c + (r ^ flip)) for r in range(16) for c in range(16)]
    return lax.ppermute(v, ("row", "col"), pairs)


def pick(v, i, axis):
    return lax.squeeze(lax.dynamic_slice_in_dim(v, i & jnp.uint32(v.shape[axis] - 1), 1, axis), (axis,))


def dot(a, b, ca, cb):
    return lax.dot_general(a, b, ((ca, cb), ((), ())), preferred_element_type=F32)


def total(own, came):
    out = own.astype(F32)
    for v in came:
        out = out + v.astype(F32)
    return out


def gather_row(v, first, later):
    near = [v] + [send_x(v, d) for d in (1, 2, 3)]
    far = swap_zlo(v)
    far = [far, send_x(far, 1), swap_zlo(near[2]), send_x(far, 3)]
    near, later, first = lax.optimization_barrier((near, later, first))
    near, far = jnp.stack(near), jnp.stack(far)
    return [near, swap_core(near), far, swap_core(far)], first, later


def swap_x(v, flip):
    return lax.ppermute(v, "row", [(i, i ^ (4 * flip)) for i in range(16)])


def swap_col(v, flip):
    return lax.ppermute(v, "col", [(i, i ^ flip) for i in range(16)])


def pair_up(v, flip):
    return jnp.concatenate([v, swap_col(v, flip)])


def gather_both(v, w, f):
    near = [v] + [send_x(v, d) for d in (1, 2, 3)]
    far = swap_zlo(v)
    w = transpose_devices(w, 0)
    far, w = lax.optimization_barrier((far, w))
    far = [far, send_x(far, 1), swap_zlo(near[2]), send_x(far, 3)]
    w = pair_up(jnp.stack([w, f])[None], 4)
    near[1], near[3], w = lax.optimization_barrier((near[1], near[3], w))
    w = pair_up(w, 8)
    near, w = lax.optimization_barrier((near, w))
    near = jnp.stack(near)
    near_swapped = swap_core(near)
    w = pair_up(w, 1)
    w, f = w[:, 0], w[:, 1]
    came = swap_col(w, 2)
    far = jnp.stack(far)
    return [near, near_swapped, far, swap_core(far)], w, came, f


def ring_start(far_block, send):
    h = far_block.shape[0] // 2
    return send(far_block[:h], 1), send(far_block[h:], 3)


def ring_end(after, before, came, send):
    h = after.shape[0] // 2
    after = jnp.concatenate([total(after[:h], [came[0]]).astype(BF16), after[h:]])
    before = jnp.concatenate([before[:h], total(before[h:], [came[1]]).astype(BF16)])
    return send(after, 1), send(before, 3)


def shards(tokens, left_proj, teacher_up, right_proj, student_gate, target):
    r, c = lax.axis_index("row").astype(jnp.uint32), lax.axis_index("col").astype(jnp.uint32)
    x, zl, k, low = r >> 2, (r >> 1) & 1, r & 1, r & 3
    zh, y = c >> 2, c & 3
    n_tok = tokens.shape[0]
    n_stu = student_gate.shape[1]
    factor = 1.0 / math.sqrt(n_tok * 16)

    def reduce_y(parts):
        parts = jnp.stack(parts)
        came = [send_y(pick(parts, (y + d) ^ low, 0), d) for d in (1, 2, 3)]
        return pick(parts, y ^ low, 0), came

    first = dot(tokens, left_proj, (1,), (0,)).astype(BF16)
    first, teach = lax.optimization_barrier((first, teacher_up))
    feat = lax.dynamic_slice_in_dim(tokens, (2 * x + k) * 256, 256, 1)
    teach, first, first_came, feat = gather_both(teach, first, feat)

    def block_products(v):
        return dot(v, right_proj, (2,), (0,)).astype(BF16)

    merged = [block_products(v) for v in teach]
    first_came, merged = lax.optimization_barrier((first_came, merged))
    first = jnp.concatenate([first, first_came])
    first = first.reshape((4, 4) + first.shape[1:])
    merged = jnp.stack(merged)
    merged_came = ring_start(pick(merged, (y + 2) ^ low, 0), send_y)

    def product(e):
        blocks = [pick(pick(first, low ^ e ^ y, 0), (x - d) ^ zh, 0) for d in range(4)]
        return dot(jnp.stack(blocks), teach[e], (0, 2), (0, 1))

    second = (product(0) + product(1) + product(2) + product(3)).astype(BF16)
    gate_pre = dot(tokens, student_gate, (1,), (0,))
    second, merged_came, feat = gather_row(second, merged_came, feat)
    merged_came = ring_end(pick(merged, (y + 1) ^ low, 0), pick(merged, (y - 1) ^ low, 0), merged_came, send_y)
    feat = pair_up(feat, 2)

    up_pre, feat = lax.optimization_barrier(([block_products(v) for v in second], feat))
    up_pre, came = reduce_y(up_pre)
    feat = [feat, swap_x(feat, 1), swap_x(feat, 3)]

    second = jnp.stack(second)
    second = [pick(pick(second, low ^ y ^ i, 0), x - (zh ^ j), 0) for i in range(4) for j in range(4)]
    second = jnp.stack(second)
    second, up_pre, came, merged_came = lax.optimization_barrier((second, up_pre, came, merged_came))

    up_pre = total(up_pre, came).astype(BF16)
    up_pre, merged_came = lax.optimization_barrier((up_pre, merged_came))
    came = [send_z(pick(up_pre, x - zh - d, 0), d) for d in (1, 2, 3)]
    merged = total(pick(merged, y ^ low, 0), merged_came).astype(BF16)
    came, merged, feat = lax.optimization_barrier((came, merged, feat))
    feat.insert(2, swap_x(feat[0], 2))
    up_pre = total(pick(up_pre, x - zh, 0), came)

    grad_up = up_gradient(gate_pre, up_pre, target, factor)
    grad_up, merged = lax.optimization_barrier((grad_up, merged))
    grad_all = jnp.stack([grad_up] + [swap_col(grad_up, 4 * j) for j in (1, 2, 3)])
    merged_came = ring_start(pick(merged, x - zh - 2, 0), send_z)
    came = [swap_col(grad_all, i) for i in (1, 2, 3)]
    came[0], merged_came, feat = lax.optimization_barrier((came[0], merged_came, feat))
    feat = jnp.stack(feat)
    feat_other = swap_core(feat)
    merged_came = ring_end(pick(merged, x - zh - 1, 0), pick(merged, x - zh + 1, 0), merged_came, send_z)
    grad_all = jnp.stack([grad_all] + came)
    grad_all = grad_all.reshape((16,) + grad_up.shape)
    merged = total(pick(merged, x - zh, 0), merged_came).astype(BF16)

    def left_part(v):
        v = v.reshape((4, 16, n_tok, -1))
        v = dot(v, grad_all, (1, 2), (0, 1)).astype(BF16)
        v = dot(v, merged, (2,), (1,)).astype(BF16)
        return v.reshape((4, 2, n_tok, -1))

    left = [left_part(feat), left_part(feat_other)]
    came = swap_core(jnp.stack([pick(left[1], 1 - k, 1), pick(left[0], 1 - k, 1)]))
    left = total(jnp.stack([pick(v, k, 1) for v in left]), [came]).astype(BF16)
    came = [swap_x(left[:, i], i) for i in (1, 2, 3)]
    left = total(left[:, 0], came).astype(BF16)

    grad_all, left = lax.optimization_barrier((grad_all, left))
    came = [transpose_devices(pick(left, zl ^ k, 0), 0), transpose_devices(pick(left, 1 - (zl ^ k), 0), 2)]
    grad_right = dot(second, grad_all, (0, 1), (0, 1))
    grad_right, came = lax.optimization_barrier((grad_right, came))
    grad_left = total(came[0], came[1:])
    return (grad_left, grad_right)


def solution(mesh):
    return jax.shard_map(
        shards,
        mesh=mesh,
        in_specs=(
            P("col", None),
            P(None, "row"),
            P("row", "col"),
            P("col", "row"),
            P(None, "row"),
            P("col", "row"),
        ),
        out_specs=(P("col", "row"), P("col", "row")),
        check_vma=False,
    )
```

```python
import math

import jax
import jax.numpy as jnp
from jax import lax
from jax.experimental.layout import Layout, with_layout_constraint
from jax.sharding import PartitionSpec as P

F32 = jnp.float32
BF16 = jnp.bfloat16


def up_gradient(gate_pre, up_pre, target, factor):
    gate_act = jax.nn.silu(gate_pre)
    return ((gate_act * up_pre - target.astype(F32)) * gate_act * factor).astype(BF16)


def send_y(v, d):
    return lax.ppermute(v, "col", [(4 * a + b, 4 * a + (b + d) % 4) for a in range(4) for b in range(4)])


def send_z(v, d):
    return lax.ppermute(v, "col", [(4 * a + b, 4 * ((a + d) % 4) + b) for a in range(4) for b in range(4)])


def send_x(v, d):
    return lax.ppermute(v, "row", [(4 * a + b, 4 * ((a + d) % 4) + b) for a in range(4) for b in range(4)])


def swap_core(v):
    return lax.ppermute(v, "row", [(i, i ^ 1) for i in range(16)])


def swap_zlo(v):
    return lax.ppermute(v, "row", [(i, i ^ 2) for i in range(16)])


def transpose_devices(v, flip):
    pairs = [(16 * r + c, 16 * c + (r ^ flip)) for r in range(16) for c in range(16)]
    return lax.ppermute(v, ("row", "col"), pairs)


def pick(v, i, axis):
    return lax.squeeze(lax.dynamic_slice_in_dim(v, i & jnp.uint32(v.shape[axis] - 1), 1, axis), (axis,))


def dot(a, b, ca, cb):
    return lax.dot_general(a, b, ((ca, cb), ((), ())), preferred_element_type=F32)


def total(own, came):
    out = own.astype(F32)
    for v in came:
        out = out + v.astype(F32)
    return out


def gather_z(v):
    return jnp.stack([v] + [send_z(v, 4 - j) for j in (1, 2, 3)])


def gather_y(v):
    return jnp.stack([v] + [send_y(v, 4 - i) for i in (1, 2, 3)])


def gather_col(v):
    return gather_y(gather_z(v))


def gather_row(v):
    near = [v] + [send_x(v, d) for d in (1, 2, 3)]
    far = swap_zlo(v)
    far = [far, send_x(far, 1), swap_zlo(near[2]), send_x(far, 3)]
    near, far = jnp.stack(near), jnp.stack(far)
    return [near, swap_core(near), far, swap_core(far)]


def swap_col(v, flip):
    return lax.ppermute(v, "col", [(i, i ^ flip) for i in range(16)])


def pair_up(v, flip):
    return jnp.concatenate([v, swap_col(v, flip)])


def gather_both(v, w):
    near = [v] + [send_x(v, d) for d in (1, 2, 3)]
    far = swap_zlo(v)
    w = transpose_devices(w, 0)[None]
    far, w = lax.optimization_barrier((far, w))
    far = [far, send_x(far, 1), swap_zlo(near[2]), send_x(far, 3)]
    w = pair_up(w, 4)
    near[1], w = lax.optimization_barrier((near[1], w))
    w = pair_up(w, 8)
    near, w = lax.optimization_barrier((near, w))
    near = jnp.stack(near)
    near_swapped = swap_core(near)
    w = pair_up(w, 1)
    far[1], w = lax.optimization_barrier((far[1], w))
    w = pair_up(w, 2)
    far = jnp.stack(far)
    return [near, near_swapped, far, swap_core(far)], w.reshape((4, 4) + w.shape[1:])


def ring_start(far_block, send):
    h = far_block.shape[0] // 2
    return send(far_block[:h], 1), send(far_block[h:], 3)


def ring_end(after, before, came, send):
    h = after.shape[0] // 2
    after = jnp.concatenate([total(after[:h], [came[0]]).astype(BF16), after[h:]])
    before = jnp.concatenate([before[:h], total(before[h:], [came[1]]).astype(BF16)])
    return send(after, 1), send(before, 3)


def shards(tokens, left_proj, teacher_up, right_proj, student_gate, target):
    r, c = lax.axis_index("row").astype(jnp.uint32), lax.axis_index("col").astype(jnp.uint32)
    x, zl, k, low = r >> 2, (r >> 1) & 1, r & 1, r & 3
    zh, y = c >> 2, c & 3
    n_tok = tokens.shape[0]
    n_stu = student_gate.shape[1]
    factor = 1.0 / math.sqrt(n_tok * 16)

    def reduce_y(parts):
        parts = jnp.stack(parts)
        came = [send_y(pick(parts, (y + d) ^ low, 0), d) for d in (1, 2, 3)]
        return pick(parts, y ^ low, 0), came

    first = dot(tokens, left_proj, (1,), (0,)).astype(BF16)
    first, teach = lax.optimization_barrier((first, teacher_up))
    teach, first = gather_both(teach, first)

    def product(e):
        blocks = [pick(pick(first, low ^ e ^ y, 0), (x - d) ^ zh, 0) for d in range(4)]
        return dot(jnp.stack(blocks), teach[e], (0, 2), (0, 1))

    def block_products(v):
        return dot(v, right_proj, (2,), (0,)).astype(BF16)

    merged = [block_products(teach[0]), block_products(teach[2])]
    second = (product(0) + product(1) + product(2) + product(3)).astype(BF16)
    second, teach = lax.optimization_barrier((second, teach))
    gate_pre = dot(tokens, student_gate, (1,), (0,))
    second = gather_row(second)

    merged = jnp.stack([merged[0], block_products(teach[1]), merged[1], block_products(teach[3])])
    merged_came = ring_start(pick(merged, (y + 2) ^ low, 0), send_y)

    up_pre, came = reduce_y([block_products(v) for v in second])

    second = jnp.stack(second)
    second = [pick(pick(second, low ^ (y + i), 0), x - zh - j, 0) for i in range(4) for j in range(4)]
    second = jnp.stack(second)
    second, up_pre, came, merged_came = lax.optimization_barrier((second, up_pre, came, merged_came))

    up_pre = total(up_pre, came).astype(BF16)
    up_pre, merged_came = lax.optimization_barrier((up_pre, merged_came))
    came = [send_z(pick(up_pre, x - zh - d, 0), d) for d in (1, 2, 3)]
    merged_came = ring_end(pick(merged, (y + 1) ^ low, 0), pick(merged, (y - 1) ^ low, 0), merged_came, send_y)
    up_pre = total(pick(up_pre, x - zh, 0), came)

    grad_up = up_gradient(gate_pre, up_pre, target, factor)
    grad_all = gather_z(grad_up)
    grad_all, merged_came = lax.optimization_barrier((grad_all, merged_came))
    came = [send_y(grad_all, 4 - i) for i in (1, 2, 3)]
    merged = total(pick(merged, y ^ low, 0), merged_came).astype(BF16)
    merged_came = [send_z(pick(merged, x - zh - d, 0), d) for d in (1, 3, 2)]
    grad_all = jnp.stack([grad_all] + came)
    merged = total(pick(merged, x - zh, 0), merged_came).astype(BF16)

    back = dot(grad_all, merged, (3,), (1,)).astype(BF16)
    back = back.reshape((2, 2) + back.shape[1:])
    bit = (k ^ y) & 1
    came = swap_core(pick(back, 1 - bit, 1))
    back = total(pick(back, bit, 1), [came]).astype(BF16)
    came = [send_x(pick(back, x + d - zh, 1), d) for d in (1, 2, 3)]
    back = total(pick(back, x - zh, 1), came).astype(BF16)
    mine = zl ^ ((y + bit) >> 1)
    back = total(
        transpose_devices(pick(back, mine, 0), 0), [transpose_devices(pick(back, 1 - mine, 0), 2)]
    ).astype(BF16)
    left = dot(tokens.reshape(n_tok, 16, -1), back, (0,), (0,)).astype(BF16)
    left = with_layout_constraint(left, Layout(major_to_minor=(0, 1, 2)))
    left = left.reshape((4, 4) + left.shape[1:])
    came = [send_y(pick(left, y + d, 1), d) for d in (1, 2, 3)]
    left = pick(left, y, 1)

    grad_all = grad_all.reshape((16,) + grad_up.shape)
    grad_all, left = lax.optimization_barrier((grad_all, left))
    grad_right = dot(second, grad_all, (0, 1), (0, 1))
    grad_right, left, came = lax.optimization_barrier((grad_right, left, came))

    left = total(left, came).astype(BF16)
    came = [send_z(pick(left, zh + d, 0), d) for d in (1, 2, 3)]
    grad_left = total(pick(left, zh, 0), came)
    return (grad_left, grad_right)


def solution(mesh):
    return jax.shard_map(
        shards,
        mesh=mesh,
        in_specs=(
            P("col", None),
            P(None, "row"),
            P("row", "col"),
            P("col", "row"),
            P(None, "row"),
            P("col", "row"),
        ),
        out_specs=(P("col", "row"), P("col", "row")),
        check_vma=False,
    )
```

```python
import math

import jax
import jax.numpy as jnp
from jax import lax
from jax.experimental.layout import Layout, with_layout_constraint
from jax.sharding import PartitionSpec as P

F32 = jnp.float32
BF16 = jnp.bfloat16


def up_gradient(gate_pre, up_pre, target, factor):
    gate_act = jax.nn.silu(gate_pre)
    return ((gate_act * up_pre - target.astype(F32)) * gate_act * factor).astype(BF16)


def send_y(v, d):
    return lax.ppermute(v, "col", [(4 * a + b, 4 * a + (b + d) % 4) for a in range(4) for b in range(4)])


def send_z(v, d):
    return lax.ppermute(v, "col", [(4 * a + b, 4 * ((a + d) % 4) + b) for a in range(4) for b in range(4)])


def send_x(v, d):
    return lax.ppermute(v, "row", [(4 * a + b, 4 * ((a + d) % 4) + b) for a in range(4) for b in range(4)])


def swap_core(v):
    return lax.ppermute(v, "row", [(i, i ^ 1) for i in range(16)])


def swap_zlo(v):
    return lax.ppermute(v, "row", [(i, i ^ 2) for i in range(16)])


def transpose_devices(v, flip):
    pairs = [(16 * r + c, 16 * c + (r ^ flip)) for r in range(16) for c in range(16)]
    return lax.ppermute(v, ("row", "col"), pairs)


def pick(v, i, axis):
    return lax.squeeze(lax.dynamic_slice_in_dim(v, i & jnp.uint32(v.shape[axis] - 1), 1, axis), (axis,))


def dot(a, b, ca, cb):
    return lax.dot_general(a, b, ((ca, cb), ((), ())), preferred_element_type=F32)


def total(own, came):
    out = own.astype(F32)
    for v in came:
        out = out + v.astype(F32)
    return out


def gather_z(v):
    return jnp.stack([v] + [send_z(v, 4 - j) for j in (1, 2, 3)])


def gather_y(v):
    return jnp.stack([v] + [send_y(v, 4 - i) for i in (1, 2, 3)])


def gather_col(v):
    return gather_y(gather_z(v))


def gather_row(v):
    near = [v] + [send_x(v, d) for d in (1, 2, 3)]
    far = swap_zlo(v)
    far = [far, send_x(far, 1), swap_zlo(near[2]), send_x(far, 3)]
    near, far = jnp.stack(near), jnp.stack(far)
    return [near, swap_core(near), far, swap_core(far)]


def swap_col(v, flip):
    return lax.ppermute(v, "col", [(i, i ^ flip) for i in range(16)])


def pair_up(v, flip):
    return jnp.concatenate([v, swap_col(v, flip)])


def gather_both(v, w):
    near = [v] + [send_x(v, d) for d in (1, 2, 3)]
    far = swap_zlo(v)
    w = transpose_devices(w, 0)[None]
    far, w = lax.optimization_barrier((far, w))
    far = [far, send_x(far, 1), swap_zlo(near[2]), send_x(far, 3)]
    w = pair_up(w, 4)
    near[1], w = lax.optimization_barrier((near[1], w))
    w = pair_up(w, 8)
    near, w = lax.optimization_barrier((near, w))
    near = jnp.stack(near)
    near_swapped = swap_core(near)
    w = pair_up(w, 1)
    far[1], w = lax.optimization_barrier((far[1], w))
    w = pair_up(w, 2)
    far = jnp.stack(far)
    return [near, near_swapped, far, swap_core(far)], w.reshape((4, 4) + w.shape[1:])


def ring_start(far_block, send):
    h = far_block.shape[0] // 2
    return send(far_block[:h], 1), send(far_block[h:], 3)


def ring_add(after, before, came):
    h = after.shape[0] // 2
    after = jnp.concatenate([total(after[:h], [came[0]]).astype(BF16), after[h:]])
    before = jnp.concatenate([before[:h], total(before[h:], [came[1]]).astype(BF16)])
    return after, before


def shards(tokens, left_proj, teacher_up, right_proj, student_gate, target):
    r, c = lax.axis_index("row").astype(jnp.uint32), lax.axis_index("col").astype(jnp.uint32)
    x, zl, k, low = r >> 2, (r >> 1) & 1, r & 1, r & 3
    zh, y = c >> 2, c & 3
    n_tok = tokens.shape[0]
    n_stu = student_gate.shape[1]
    factor = 1.0 / math.sqrt(n_tok * 16)

    def reduce_y(parts):
        parts = jnp.stack(parts)
        came = [send_y(pick(parts, (y + d) ^ low, 0), d) for d in (1, 2, 3)]
        return pick(parts, y ^ low, 0), came

    first = dot(tokens, left_proj, (1,), (0,)).astype(BF16)
    first, teach = lax.optimization_barrier((first, teacher_up))
    teach, first = gather_both(teach, first)

    def product(e):
        blocks = [pick(pick(first, low ^ e ^ y, 0), (x - d) ^ zh, 0) for d in range(4)]
        return dot(jnp.stack(blocks), teach[e], (0, 2), (0, 1))

    def block_products(v):
        return dot(v, right_proj, (2,), (0,)).astype(BF16)

    merged = [block_products(teach[0]), block_products(teach[2])]
    second = (product(0) + product(1) + product(2) + product(3)).astype(BF16)
    second, teach = lax.optimization_barrier((second, teach))
    gate_pre = dot(tokens, student_gate, (1,), (0,))
    second = gather_row(second)

    merged = jnp.stack([merged[0], block_products(teach[1]), merged[1], block_products(teach[3])])
    merged_came = ring_start(pick(merged, (y + 2) ^ low, 0), send_y)

    up_pre, came = reduce_y([block_products(v) for v in second])

    second = jnp.stack(second)
    second = [pick(pick(second, low ^ (y + i), 0), x - zh - j, 0) for i in range(4) for j in range(4)]
    second = jnp.stack(second)
    came[0], merged_came = lax.optimization_barrier((came[0], merged_came))
    after, before = ring_add(pick(merged, (y + 1) ^ low, 0), pick(merged, (y - 1) ^ low, 0), merged_came)
    second, up_pre, came, after, before = lax.optimization_barrier((second, up_pre, came, after, before))

    up_pre = total(up_pre, came).astype(BF16)
    up_pre, after, before = lax.optimization_barrier((up_pre, after, before))
    came = [send_z(pick(up_pre, x - zh - d, 0), d) for d in (1, 2, 3)]
    merged_came = send_y(after, 1), send_y(before, 3)
    up_pre = total(pick(up_pre, x - zh, 0), came)

    grad_up = up_gradient(gate_pre, up_pre, target, factor)
    came = [send_z(grad_up, 4 - j) for j in (1, 2, 3)]
    came[0], merged_came = lax.optimization_barrier((came[0], merged_came))
    merged = total(pick(merged, y ^ low, 0), merged_came).astype(BF16)
    came, merged = lax.optimization_barrier((came, merged))
    grad_all = jnp.stack([grad_up] + came)
    merged_came = [send_z(pick(merged, x - zh - d, 0), d) for d in (1, 3, 2)]
    grad_all = gather_y(grad_all)
    merged = total(pick(merged, x - zh, 0), merged_came).astype(BF16)

    back = dot(grad_all, merged, (3,), (1,)).astype(BF16)
    back = back.reshape((2, 2) + back.shape[1:])
    bit = (k ^ y) & 1
    came = swap_core(pick(back, 1 - bit, 1))
    back = total(pick(back, bit, 1), [came]).astype(BF16)
    came = [send_x(pick(back, x + d - zh, 1), d) for d in (1, 2, 3)]
    back = total(pick(back, x - zh, 1), came).astype(BF16)
    mine = zl ^ ((y + bit) >> 1)
    back = total(
        transpose_devices(pick(back, mine, 0), 0), [transpose_devices(pick(back, 1 - mine, 0), 2)]
    ).astype(BF16)
    left = dot(tokens.reshape(n_tok, 16, -1), back, (0,), (0,)).astype(BF16)
    left = with_layout_constraint(left, Layout(major_to_minor=(0, 1, 2)))
    left = left.reshape((4, 4) + left.shape[1:])
    came = [send_y(pick(left, y + d, 1), d) for d in (1, 2, 3)]
    left = pick(left, y, 1)

    grad_all = grad_all.reshape((16,) + grad_up.shape)
    grad_all, left = lax.optimization_barrier((grad_all, left))
    grad_right = dot(second, grad_all, (0, 1), (0, 1))
    grad_right, left, came = lax.optimization_barrier((grad_right, left, came))

    left = total(left, came).astype(BF16)
    came = [send_z(pick(left, zh + d, 0), d) for d in (1, 2, 3)]
    grad_left = total(pick(left, zh, 0), came)
    return (grad_left, grad_right)


def solution(mesh):
    return jax.shard_map(
        shards,
        mesh=mesh,
        in_specs=(
            P("col", None),
            P(None, "row"),
            P("row", "col"),
            P("col", "row"),
            P(None, "row"),
            P("col", "row"),
        ),
        out_specs=(P("col", "row"), P("col", "row")),
        check_vma=False,
    )
```

```python
import math

import jax
import jax.numpy as jnp
from jax import lax
from jax.experimental.layout import Layout, with_layout_constraint
from jax.sharding import PartitionSpec as P

F32 = jnp.float32
BF16 = jnp.bfloat16


def up_gradient(gate_pre, up_pre, target, factor):
    gate_act = jax.nn.silu(gate_pre)
    return ((gate_act * up_pre - target.astype(F32)) * gate_act * factor).astype(BF16)


def send_y(v, d):
    return lax.ppermute(v, "col", [(4 * a + b, 4 * a + (b + d) % 4) for a in range(4) for b in range(4)])


def send_z(v, d):
    return lax.ppermute(v, "col", [(4 * a + b, 4 * ((a + d) % 4) + b) for a in range(4) for b in range(4)])


def send_x(v, d):
    return lax.ppermute(v, "row", [(4 * a + b, 4 * ((a + d) % 4) + b) for a in range(4) for b in range(4)])


def swap_core(v):
    return lax.ppermute(v, "row", [(i, i ^ 1) for i in range(16)])


def swap_zlo(v):
    return lax.ppermute(v, "row", [(i, i ^ 2) for i in range(16)])


def transpose_devices(v, flip):
    pairs = [(16 * r + c, 16 * c + (r ^ flip)) for r in range(16) for c in range(16)]
    return lax.ppermute(v, ("row", "col"), pairs)


def pick(v, i, axis):
    return lax.squeeze(lax.dynamic_slice_in_dim(v, i & jnp.uint32(v.shape[axis] - 1), 1, axis), (axis,))


def dot(a, b, ca, cb):
    return lax.dot_general(a, b, ((ca, cb), ((), ())), preferred_element_type=F32)


def total(own, came):
    out = own.astype(F32)
    for v in came:
        out = out + v.astype(F32)
    return out


def gather_z(v):
    return jnp.stack([v] + [send_z(v, 4 - j) for j in (1, 2, 3)])


def gather_y(v):
    return jnp.stack([v] + [send_y(v, 4 - i) for i in (1, 2, 3)])


def gather_col(v):
    return gather_y(gather_z(v))


def gather_row(v):
    near = [v] + [send_x(v, d) for d in (1, 2, 3)]
    far = swap_zlo(v)
    far = [far, send_x(far, 1), swap_zlo(near[2]), send_x(far, 3)]
    near, far = jnp.stack(near), jnp.stack(far)
    return [near, swap_core(near), far, swap_core(far)]


def swap_col(v, flip):
    return lax.ppermute(v, "col", [(i, i ^ flip) for i in range(16)])


def pair_up(v, flip):
    return jnp.concatenate([v, swap_col(v, flip)])


def gather_both(v, w):
    near = [v] + [send_x(v, d) for d in (1, 2, 3)]
    far = swap_zlo(v)
    w = transpose_devices(w, 0)[None]
    far, w = lax.optimization_barrier((far, w))
    far = [far, send_x(far, 1), swap_zlo(near[2]), send_x(far, 3)]
    w = pair_up(w, 4)
    near[1], w = lax.optimization_barrier((near[1], w))
    w = pair_up(w, 8)
    near, w = lax.optimization_barrier((near, w))
    near = jnp.stack(near)
    near_swapped = swap_core(near)
    w = pair_up(w, 1)
    far[1], w = lax.optimization_barrier((far[1], w))
    w = pair_up(w, 2)
    return near, near_swapped, far, w.reshape((4, 4) + w.shape[1:])


def ring_start(far_block, send):
    h = far_block.shape[0] // 2
    return send(far_block[:h], 1), send(far_block[h:], 3)


def ring_add(after, before, came):
    h = after.shape[0] // 2
    after = jnp.concatenate([total(after[:h], [came[0]]).astype(BF16), after[h:]])
    before = jnp.concatenate([before[:h], total(before[h:], [came[1]]).astype(BF16)])
    return after, before


def shards(tokens, left_proj, teacher_up, right_proj, student_gate, target):
    r, c = lax.axis_index("row").astype(jnp.uint32), lax.axis_index("col").astype(jnp.uint32)
    x, zl, k, low = r >> 2, (r >> 1) & 1, r & 1, r & 3
    zh, y = c >> 2, c & 3
    n_tok = tokens.shape[0]
    n_stu = student_gate.shape[1]
    factor = 1.0 / math.sqrt(n_tok * 16)

    def reduce_y(parts):
        parts = jnp.stack(parts)
        came = [send_y(pick(parts, (y + d) ^ low, 0), d) for d in (1, 2, 3)]
        return pick(parts, y ^ low, 0), came

    first = dot(tokens, left_proj, (1,), (0,)).astype(BF16)
    first, teach = lax.optimization_barrier((first, teacher_up))
    near, near_swapped, far, first = gather_both(teach, first)

    def product(e, v):
        blocks = [pick(pick(first, low ^ e ^ y, 0), (x - d) ^ zh, 0) for d in range(4)]
        return dot(jnp.stack(blocks), v, (0, 2), (0, 1))

    def block_products(v):
        return dot(v, right_proj, (2,), (0,)).astype(BF16)

    merged = [block_products(near), block_products(near_swapped)]
    first, merged = lax.optimization_barrier((first, merged))
    second = product(0, near)
    far, second = lax.optimization_barrier((far, second))
    far = jnp.stack(far)
    teach = [near, near_swapped, far, swap_core(far)]
    second = (second + product(2, far) + product(1, near_swapped) + product(3, teach[3])).astype(BF16)
    second, teach = lax.optimization_barrier((second, teach))
    gate_pre = dot(tokens, student_gate, (1,), (0,))
    second = gather_row(second)

    merged = jnp.stack(merged + [block_products(v) for v in teach[2:]])
    merged_came = ring_start(pick(merged, (y + 2) ^ low, 0), send_y)

    up_pre, came = reduce_y([block_products(v) for v in second])

    second = jnp.stack(second)
    second = [pick(pick(second, low ^ (y + i), 0), x - zh - j, 0) for i in range(4) for j in range(4)]
    second = jnp.stack(second)
    came[0], merged_came = lax.optimization_barrier((came[0], merged_came))
    after, before = ring_add(pick(merged, (y + 1) ^ low, 0), pick(merged, (y - 1) ^ low, 0), merged_came)
    second, up_pre, came, after, before = lax.optimization_barrier((second, up_pre, came, after, before))

    up_pre = total(up_pre, came).astype(BF16)
    up_pre, after, before = lax.optimization_barrier((up_pre, after, before))
    came = [send_z(pick(up_pre, x - zh - d, 0), d) for d in (1, 2, 3)]
    merged_came = send_y(after, 1), send_y(before, 3)
    up_pre = total(pick(up_pre, x - zh, 0), came)

    grad_up = up_gradient(gate_pre, up_pre, target, factor)
    came = [send_z(grad_up, 4 - j) for j in (1, 2, 3)]
    came[0], merged_came = lax.optimization_barrier((came[0], merged_came))
    merged = total(pick(merged, y ^ low, 0), merged_came).astype(BF16)
    came, merged = lax.optimization_barrier((came, merged))
    grad_all = jnp.stack([grad_up] + came)
    merged_came = [send_z(pick(merged, x - zh - d, 0), d) for d in (1, 3, 2)]
    grad_all = gather_y(grad_all)
    merged = total(pick(merged, x - zh, 0), merged_came).astype(BF16)

    back = dot(grad_all, merged, (3,), (1,)).astype(BF16)
    back = back.reshape((2, 2) + back.shape[1:])
    bit = (k ^ y) & 1
    came = swap_core(pick(back, 1 - bit, 1))
    back = total(pick(back, bit, 1), [came]).astype(BF16)
    came = [send_x(pick(back, x + d - zh, 1), d) for d in (1, 2, 3)]
    back = total(pick(back, x - zh, 1), came).astype(BF16)
    mine = zl ^ ((y + bit) >> 1)
    back = total(
        transpose_devices(pick(back, mine, 0), 0), [transpose_devices(pick(back, 1 - mine, 0), 2)]
    ).astype(BF16)
    left = dot(tokens.reshape(n_tok, 16, -1), back, (0,), (0,)).astype(BF16)
    left = with_layout_constraint(left, Layout(major_to_minor=(0, 1, 2)))
    left = left.reshape((4, 4) + left.shape[1:])
    came = [send_y(pick(left, y + d, 1), d) for d in (1, 2, 3)]
    left = pick(left, y, 1)

    grad_all = grad_all.reshape((16,) + grad_up.shape)
    grad_all, left = lax.optimization_barrier((grad_all, left))
    grad_right = dot(second, grad_all, (0, 1), (0, 1))
    grad_right, left, came = lax.optimization_barrier((grad_right, left, came))

    left = total(left, came).astype(BF16)
    came = [send_z(pick(left, zh + d, 0), d) for d in (1, 2, 3)]
    grad_left = total(pick(left, zh, 0), came)
    return (grad_left, grad_right)


def solution(mesh):
    return jax.shard_map(
        shards,
        mesh=mesh,
        in_specs=(
            P("col", None),
            P(None, "row"),
            P("row", "col"),
            P("col", "row"),
            P(None, "row"),
            P("col", "row"),
        ),
        out_specs=(P("col", "row"), P("col", "row")),
        check_vma=False,
    )
```

```python
import math

import jax
import jax.numpy as jnp
from jax import lax
from jax.experimental.layout import Layout, with_layout_constraint
from jax.sharding import PartitionSpec as P

F32 = jnp.float32
BF16 = jnp.bfloat16


def up_gradient(gate_pre, up_pre, target, factor):
    gate_act = jax.nn.silu(gate_pre)
    return ((gate_act * up_pre - target.astype(F32)) * gate_act * factor).astype(BF16)


def send_y(v, d):
    return lax.ppermute(v, "col", [(4 * a + b, 4 * a + (b + d) % 4) for a in range(4) for b in range(4)])


def send_z(v, d):
    return lax.ppermute(v, "col", [(4 * a + b, 4 * ((a + d) % 4) + b) for a in range(4) for b in range(4)])


def send_x(v, d):
    return lax.ppermute(v, "row", [(4 * a + b, 4 * ((a + d) % 4) + b) for a in range(4) for b in range(4)])


def swap_core(v):
    return lax.ppermute(v, "row", [(i, i ^ 1) for i in range(16)])


def swap_zlo(v):
    return lax.ppermute(v, "row", [(i, i ^ 2) for i in range(16)])


def transpose_devices(v, flip):
    pairs = [(16 * r + c, 16 * c + (r ^ flip)) for r in range(16) for c in range(16)]
    return lax.ppermute(v, ("row", "col"), pairs)


def pick(v, i, axis):
    return lax.squeeze(lax.dynamic_slice_in_dim(v, i & jnp.uint32(v.shape[axis] - 1), 1, axis), (axis,))


def dot(a, b, ca, cb):
    return lax.dot_general(a, b, ((ca, cb), ((), ())), preferred_element_type=F32)


def total(own, came):
    out = own.astype(F32)
    for v in came:
        out = out + v.astype(F32)
    return out


def gather_z(v):
    return jnp.stack([v] + [send_z(v, 4 - j) for j in (1, 2, 3)])


def gather_y(v):
    return jnp.stack([v] + [send_y(v, 4 - i) for i in (1, 2, 3)])


def gather_col(v):
    return gather_y(gather_z(v))


def gather_row(v):
    near = [v] + [send_x(v, d) for d in (1, 2, 3)]
    far = swap_zlo(v)
    far = [far, send_x(far, 1), swap_zlo(near[2]), send_x(far, 3)]
    near, far = jnp.stack(near), jnp.stack(far)
    return [near, swap_core(near), far, swap_core(far)]


def swap_col(v, flip):
    return lax.ppermute(v, "col", [(i, i ^ flip) for i in range(16)])


def pair_up(v, flip):
    return jnp.concatenate([v, swap_col(v, flip)])


def gather_both(v, w):
    near = [v] + [send_x(v, d) for d in (1, 2, 3)]
    far = swap_zlo(v)
    w = transpose_devices(w, 0)[None]
    far, w = lax.optimization_barrier((far, w))
    far = [far, send_x(far, 1), swap_zlo(near[2]), send_x(far, 3)]
    w = pair_up(w, 4)
    near[1], w = lax.optimization_barrier((near[1], w))
    w = pair_up(w, 8)
    near, w = lax.optimization_barrier((near, w))
    near = jnp.stack(near)
    near_swapped = swap_core(near)
    w = pair_up(w, 1)
    far[1], w = lax.optimization_barrier((far[1], w))
    w = pair_up(w, 2)
    far = jnp.stack(far)
    return [near, near_swapped, far, swap_core(far)], w.reshape((4, 4) + w.shape[1:])


def ring_start(far_block, send):
    h = far_block.shape[0] // 2
    return send(far_block[:h], 1), send(far_block[h:], 3)


def ring_add(after, before, came):
    h = after.shape[0] // 2
    after = jnp.concatenate([total(after[:h], [came[0]]).astype(BF16), after[h:]])
    before = jnp.concatenate([before[:h], total(before[h:], [came[1]]).astype(BF16)])
    return after, before


def shards(tokens, left_proj, teacher_up, right_proj, student_gate, target):
    r, c = lax.axis_index("row").astype(jnp.uint32), lax.axis_index("col").astype(jnp.uint32)
    x, zl, k, low = r >> 2, (r >> 1) & 1, r & 1, r & 3
    zh, y = c >> 2, c & 3
    n_tok = tokens.shape[0]
    n_stu = student_gate.shape[1]
    factor = 1.0 / math.sqrt(n_tok * 16)

    def reduce_y(parts):
        parts = jnp.stack(parts)
        came = [send_y(pick(parts, (y + d) ^ low, 0), d) for d in (1, 2, 3)]
        return pick(parts, y ^ low, 0), came

    first = dot(tokens, left_proj, (1,), (0,)).astype(BF16)
    first, teach = lax.optimization_barrier((first, teacher_up))
    teach, first = gather_both(teach, first)

    def product(e):
        blocks = [pick(pick(first, low ^ e ^ y, 0), (x - d) ^ zh, 0) for d in range(4)]
        return dot(jnp.stack(blocks), teach[e], (0, 2), (0, 1))

    def block_products(v):
        return dot(v, right_proj, (2,), (0,)).astype(BF16)

    merged = [block_products(teach[0]), block_products(teach[2])]
    second = (product(0) + product(1) + product(2) + product(3)).astype(BF16)
    second, teach = lax.optimization_barrier((second, teach))
    gate_pre = dot(tokens, student_gate, (1,), (0,))
    second = gather_row(second)

    merged = jnp.stack([merged[0], block_products(teach[1]), merged[1], block_products(teach[3])])
    merged_came = ring_start(pick(merged, (y + 2) ^ low, 0), send_y)

    up_pre, came = reduce_y([block_products(v) for v in second])

    second = jnp.stack(second)
    second = [pick(pick(second, low ^ (y + i), 0), x - zh - j, 0) for i in range(4) for j in range(4)]
    second = jnp.stack(second)
    came[0], merged_came = lax.optimization_barrier((came[0], merged_came))
    after, before = ring_add(pick(merged, (y + 1) ^ low, 0), pick(merged, (y - 1) ^ low, 0), merged_came)
    second, up_pre, came, after, before = lax.optimization_barrier((second, up_pre, came, after, before))

    up_pre = total(up_pre, came).astype(BF16)
    up_pre, after, before = lax.optimization_barrier((up_pre, after, before))
    came = [send_z(pick(up_pre, x - zh - d, 0), d) for d in (1, 2, 3)]
    merged_came = send_y(after, 1), send_y(before, 3)
    up_pre = total(pick(up_pre, x - zh, 0), came)

    grad_up = up_gradient(gate_pre, up_pre, target, factor)
    came = [send_z(grad_up, 4 - j) for j in (1, 2, 3)]
    came[0], merged_came = lax.optimization_barrier((came[0], merged_came))
    merged = total(pick(merged, y ^ low, 0), merged_came).astype(BF16)
    came, merged = lax.optimization_barrier((came, merged))
    grad_all = jnp.stack([grad_up] + came)
    merged_came = [send_z(pick(merged, x - zh - d, 0), d) for d in (2, 1, 3)]
    grad_all = gather_y(grad_all)
    merged = total(pick(merged, x - zh, 0), merged_came).astype(BF16)

    back = dot(grad_all, merged, (3,), (1,)).astype(BF16)
    back = back.reshape((2, 2) + back.shape[1:])
    bit = (k ^ y) & 1
    came = swap_core(pick(back, 1 - bit, 1))
    back = total(pick(back, bit, 1), [came]).astype(BF16)
    came = [send_x(pick(back, x + d - zh, 1), d) for d in (1, 2, 3)]
    back = total(pick(back, x - zh, 1), came).astype(BF16)
    mine = zl ^ ((y + bit) >> 1)
    back = total(
        transpose_devices(pick(back, mine, 0), 0), [transpose_devices(pick(back, 1 - mine, 0), 2)]
    ).astype(BF16)
    left = dot(tokens.reshape(n_tok, 16, -1), back, (0,), (0,)).astype(BF16)
    left = with_layout_constraint(left, Layout(major_to_minor=(0, 1, 2)))
    left = left.reshape((4, 4) + left.shape[1:])
    came = [send_y(pick(left, y + d, 1), d) for d in (1, 2, 3)]
    left = pick(left, y, 1)

    grad_all = grad_all.reshape((16,) + grad_up.shape)
    grad_all, left = lax.optimization_barrier((grad_all, left))
    grad_right = dot(second, grad_all, (0, 1), (0, 1))
    grad_right, left, came = lax.optimization_barrier((grad_right, left, came))

    left = total(left, came).astype(BF16)
    came = [send_z(pick(left, zh + d, 0), d) for d in (1, 2, 3)]
    grad_left = total(pick(left, zh, 0), came)
    return (grad_left, grad_right)


def solution(mesh):
    return jax.shard_map(
        shards,
        mesh=mesh,
        in_specs=(
            P("col", None),
            P(None, "row"),
            P("row", "col"),
            P("col", "row"),
            P(None, "row"),
            P("col", "row"),
        ),
        out_specs=(P("col", "row"), P("col", "row")),
        check_vma=False,
    )
```
